32 devices in a mesh: seg: 4 (over z), blk: 8 (over y, x, core).
Axes of the slice: x: 2, y: 2, z: 4, core: 2. Of those that a mesh axis runs over, the one named last changes fastest.
Arguments:
- train_acts: bfloat16 [4, 1024, 512], P('seg', 'blk'), may hold values from -6 to 6
- train_grads: bfloat16 [4, 1024, 4096], P('seg', 'blk'), may hold values from -0.0059814453 to 0.0059814453
- counts: int32 [8], replicated, may hold values from 1 to 2, as said below
- basis_in: bfloat16 [4, 1, 512, 512], P('seg'), may hold values from -1 to 1, as said below
- basis_out: bfloat16 [4, 8, 512, 512], P('seg', 'blk'), may hold values from -1 to 1, as said below
- eigenvalues: bfloat16 [4, 8, 512, 512], P('seg', 'blk'), may hold values from 0.049804688 to 5
- back_weight: bfloat16 [4, 8, 512, 512], P('seg', 'blk'), may hold values from -0.25 to 0.25
- derivative: bfloat16 [4, 4, 32, 4096], P('seg', None, None, 'blk'), may hold values from 0 to 1
- query_acts: bfloat16 [4, 4, 32, 512], P('seg'), may hold values from -6 to 6
- query_top: bfloat16 [4, 32, 4096], P(None, None, 'blk'), may hold values from -0.0059814453 to 0.0059814453
Outputs:
- scores: float32 [4, 16], P(None, 'blk')
The draws below stay inside these ranges and needn't reach their ends.
Inputs may be any that keep to these rules, and one draw needn't show every extreme that they name: In each pair of indices 2k and 2k+1 of blk one count is 2 and the other 1, so all counts add up to 12; slots below a device's count are valid. `basis_in`: each 512 x 512 matrix is orthogonal up to rounding. `basis_out`: each 512 x 512 matrix is orthogonal up to rounding.
All inputs are finite; a program needn't handle non-finite values.
Results may differ from the reference program's by a relative error of at most 0.015.
Values may be sent and summed in bfloat16 or wider, within the bound.
A program may use at most 64 MiB of HBM per device.

```python
import math
import jax
import jax.numpy as jnp
from jax import lax

D_BLK = 512
IN_SL = 1
QUERIES = 4
QT = 32
TB = 64
SLOTS = 2
SEGS = 4
OUT_SL = 8
IN = 512
OUT = 4096
TOKENS = 1024


def draw_counts(key, part):
    which = jax.random.randint(jax.random.fold_in(key, 37), (OUT_SL // 2,), 0, 2).astype(jnp.int32)
    paired = jnp.stack([1 + which, 2 - which], axis=1)
    return paired.reshape(OUT_SL).astype(jnp.int32)


def draw_basis_in(key, part):
    raw = jax.random.normal(jax.random.fold_in(key, 11), (SEGS, IN_SL, D_BLK, D_BLK), jnp.float32)
    ortho, upper = jnp.linalg.qr(raw)
    return ortho.astype(jnp.bfloat16)


def draw_basis_out(key, part):
    raw = jax.random.normal(jax.random.fold_in(key, 23), (SEGS, OUT_SL, D_BLK, D_BLK), jnp.float32)
    ortho, upper = jnp.linalg.qr(raw)
    return ortho.astype(jnp.bfloat16)


def level_of(own_key, dims, pieces, least, largest):
    level = 1.0
    for position, blocks in pieces:
        heights = jax.random.uniform(jax.random.fold_in(jax.random.fold_in(own_key, 6), position), (blocks,), jnp.float32, least / len(pieces), largest / len(pieces))
        level = level * jnp.repeat(jnp.exp(heights), dims[position] // blocks).reshape((-1,) + (1,) * (len(dims) - 1 - position))
    return level


def normal_values(rng, shape, scale, bound, split=(), held_as=jnp.bfloat16):
    gain = level_of(rng, shape, split, -0.22, 0.18) if split else 1.0
    drawn = jax.random.normal(rng, shape, jnp.float32) * scale * gain
    return jnp.minimum(jnp.maximum(drawn, -bound), bound).astype(held_as)


def setup_inputs(seed: int = 0) -> dict:
    seeds = jax.random.split(jax.random.key(seed), 11)
    train_acts = normal_values(seeds[0], (SEGS, TOKENS, IN), 1.0, 6.0, ((0, 4), (1, 8)))
    train_grads = normal_values(seeds[1], (SEGS, TOKENS, OUT), 0.001, 0.0059814453, ((0, 4), (1, 8)))
    counts = draw_counts(jax.random.fold_in(seeds[10], 71), 0)
    basis_in = draw_basis_in(jax.random.fold_in(seeds[10], 71), 0)
    basis_out = draw_basis_out(jax.random.fold_in(seeds[10], 71), 0)
    eigenvalues = jnp.clip(jnp.exp(math.log(5.0) - 4.609084 * jax.random.uniform(seeds[5], (SEGS, OUT_SL, D_BLK, IN), jnp.float32) ** level_of(seeds[5], (SEGS, OUT_SL, D_BLK, IN), ((0, 4), (1, 8)), -0.2, 0.2)), 0.049804688, 5.0).astype(jnp.bfloat16)
    back_weight = normal_values(seeds[6], (SEGS, OUT_SL, D_BLK, D_BLK), D_BLK ** -0.5, 0.25, ((0, 4), (1, 8)))
    derivative = jnp.clip(1.0 * jax.random.uniform(seeds[7], (SEGS, QUERIES, QT, OUT), jnp.float32) ** level_of(seeds[7], (SEGS, QUERIES, QT, OUT), ((0, 4), (3, 8)), -0.2, 0.2), 0.0, 1.0).astype(jnp.bfloat16)
    query_acts = normal_values(seeds[8], (SEGS, QUERIES, QT, IN), 1.0, 6.0, ((0, 4),))
    query_top = normal_values(seeds[9], (QUERIES, QT, OUT), 0.001, 0.0059814453, ((2, 8),))
    return dict(train_acts=train_acts, train_grads=train_grads, counts=counts, basis_in=basis_in, basis_out=basis_out, eigenvalues=eigenvalues, back_weight=back_weight, derivative=derivative, query_acts=query_acts, query_top=query_top)


damping = 0.05

def reference(train_acts, train_grads, counts, basis_in, basis_out, eigenvalues, back_weight, derivative, query_acts, query_top):
    f32 = jnp.float32
    b16 = jnp.bfloat16
    seg_count = train_acts.shape[0]
    queries, query_tok, out_width = query_top.shape
    blk_width = basis_out.shape[-1]
    out_slices = basis_out.shape[1]
    in_slices = basis_in.shape[1]
    in_width = in_slices * blk_width
    n_slot = train_acts.shape[1] // TB
    current = query_top
    errors = [current]
    for segment in range(seg_count - 1, 0, -1):
        shaped = current.reshape(queries, query_tok, out_slices, blk_width).astype(f32)
        mixed = jnp.einsum('qtod,ode->qtoe', shaped, back_weight[segment].astype(f32))
        mixed = mixed.reshape(queries, query_tok, out_width)
        current = (current.astype(f32) + mixed * derivative[segment].astype(f32)).astype(b16)
        errors.insert(0, current)
    errors = jnp.stack(errors)

    def per_segment(operands):
        error_seg, acts_seg, inner_basis, outer_basis, eigen_seg, grads_train, acts_train = operands
        err_split = error_seg.reshape(queries, query_tok, out_slices, blk_width).astype(f32)
        rot_err = jnp.einsum('qtod,ode->qtoe', err_split, outer_basis.astype(f32)).astype(b16)
        act_split = acts_seg.reshape(queries, query_tok, in_slices, blk_width).astype(f32)
        rot_acts = jnp.einsum('qtid,ide->qtie', act_split, inner_basis.astype(f32)).astype(b16)
        core_raw = jnp.einsum('qtod,qtie->qodie', rot_err.astype(f32), rot_acts.astype(f32))
        core_raw = core_raw.reshape(queries, out_slices, blk_width, in_width)
        scaled_core = (core_raw / (eigen_seg.astype(f32)[None] + damping)).astype(b16)
        left_prod = jnp.einsum('ocd,qodf->qocf', outer_basis.astype(f32), scaled_core.astype(f32)).astype(b16)
        left_split = left_prod.reshape(queries, out_slices, blk_width, in_slices, blk_width)
        precond = jnp.einsum('qocie,ife->qocif', left_split.astype(f32), inner_basis.astype(f32))
        precond = precond.reshape(queries, out_slices, blk_width, in_width).astype(b16)
        act_slots = acts_train.reshape(n_slot, TB, in_width).astype(f32)
        grad_split = jnp.moveaxis(grads_train.reshape(n_slot * TB, out_slices, blk_width), 1, 0)
        precond_split = jnp.moveaxis(precond, 1, 0)

        def per_slice(slice_ops):
            grads_slice, precond_slice = slice_ops
            grad_slots = grads_slice.reshape(n_slot, TB, blk_width).astype(f32)
            outer_prod = jnp.einsum('ntd,nte->nde', grad_slots, act_slots).astype(b16)
            return jnp.einsum('nde,qde->qn', outer_prod.astype(f32), precond_slice.astype(f32))
        return jnp.sum(lax.map(per_slice, (grad_split, precond_split)), axis=0)
    seg_scores = lax.map(per_segment, (errors, query_acts, basis_in, basis_out, eigenvalues, train_grads, train_acts))
    summed = jnp.sum(seg_scores, axis=0)
    slot_ids = jnp.arange(n_slot, dtype=jnp.int32)
    valid = slot_ids % SLOTS < jnp.take(counts, slot_ids // SLOTS)
    return summed * valid.astype(f32)[None, :]
```

```python
import functools

import jax
import jax.numpy as jnp
from jax import lax
from jax.experimental import pallas as pl
from jax.experimental.pallas import tpu as pltpu
from jax.sharding import PartitionSpec as P

SLOTS = 2
HALVES = 2
damping = 0.05
F32 = jnp.float32
B16 = jnp.bfloat16
MESH = pl.DeviceIdType.MESH


def kernel(
    segs,
    blks,
    queries,
    counts_h,
    acts_h,
    grads_h,
    bin_h,
    bout_h,
    eig_h,
    back_h,
    deriv_h,
    qacts_h,
    qtop_h,
    out,
    counts,
    acts,
    own_g,
    other_g,
    other_a,
    b_in,
    b_out,
    eig,
    back,
    deriv,
    qacts,
    errs,
    moved,
    rot_q,
    core_all,
    grads0,
    grads1,
    racts,
    part,
    packed,
    gathered,
    load_sem,
    sel_recv,
    g0_send,
    g0_recv,
    g1_send,
    g1_recv,
    a_send,
    a_recv,
    am_recv,
    e_send,
    e_recv,
    p_send,
    p_recv,
    ready,
):
    seg = lax.axis_index("seg")
    blk = lax.axis_index("blk")
    chips = blks // 2
    steps = chips.bit_length() - 1
    chip = blk // 2
    lane = blk % 2
    mate_lane = 1 - lane
    mate = chip * 2 + mate_lane
    rows = acts_h.shape[0]
    tb = rows // SLOTS
    half = tb // 2
    block = tb + half
    width = bin_h.shape[0]
    qrows = qtop_h.shape[0]
    qt = qrows // queries
    piece = qrows // HALVES

    barrier = pltpu.get_barrier_semaphore()
    for off in range(1, blks):
        pl.semaphore_signal(
            barrier, inc=1, device_id=(seg, lax.rem(blk + off, blks)), device_id_type=MESH
        )
    for off in range(1, segs):
        pl.semaphore_signal(
            barrier, inc=1, device_id=(lax.rem(seg + off, segs), blk), device_id_type=MESH
        )

    def flip(c, bit):
        return c + bit * (1 - 2 * lax.rem(c // bit, 2))

    def chip_at(off):
        c = chip
        for j in range(steps):
            if off >> j & 1:
                c = flip(c, 1 << j)
        return c

    low = [1 << j for j in range(steps)]
    high = low[::-1]
    bits = [a + lane * (b - a) for a, b in zip(low, high)]
    partners = [flip(chip, a) + lane * (flip(chip, b) - flip(chip, a)) for a, b in zip(low, high)]

    def slot_of(code):
        return sum((bits[j] for j in range(steps) if code >> j & 1), 0)

    def remote(src, dst, ssem, rsem, seg_to, blk_to):
        return pltpu.make_async_remote_copy(
            src_ref=src,
            dst_ref=dst,
            send_sem=ssem,
            recv_sem=rsem,
            device_id=(seg_to, blk_to),
            device_id_type=MESH,
        )

    def cols(index):
        return pl.ds(pl.multiple_of(index * width, width), width)

    def span(index, size):
        return pl.ds(pl.multiple_of(index * size, size), size)

    def landed(ref, sem):
        remote(ref, ref, g0_send, sem, seg, mate).wait_recv()

    def loaded(ref, sem):
        pltpu.make_async_copy(ref, ref, sem).wait()

    def racts_at(slot, side):
        return racts.at[span(slot * 2 + side, block)]

    keep = pl.ds(pl.multiple_of(tb + lane * half, half), half)
    give = pl.ds(pl.multiple_of(tb + mate_lane * half, half), half)

    l_top = pltpu.make_async_copy(qtop_h, errs, load_sem.at[0])

    @pl.when(seg == segs - 1)
    def _():
        l_top.start()

    for src, dst, n in (
        (back_h, back, 1),
        (deriv_h, deriv, 1),
        (acts_h, acts, 2),
        (bin_h, b_in, 2),
        (counts_h, counts, 3),
        (grads_h.at[keep, :], own_g, 4),
        (bout_h, b_out, 5),
        (qacts_h, qacts, 5),
        (eig_h, eig, 6),
        (grads_h.at[pl.ds(0, tb), cols(blk)], grads0.at[span(lane, tb)], None),
    ):
        sem = g0_recv.at[0] if n is None else load_sem.at[n]
        pltpu.make_async_copy(src, dst, sem).start()

    def e_copy(n):
        r = pl.ds(n * piece, piece)
        below = lax.rem(seg + segs - 1, segs)
        return remote(moved.at[r], errs.at[r], e_send, e_recv.at[n], below, blk)

    def advance(n):
        r = pl.ds(n * piece, piece)
        e = errs[r]
        mixed = jnp.dot(e, back[...], preferred_element_type=F32)
        moved[r] = (e.astype(F32) + mixed * deriv[r].astype(F32)).astype(B16)

    @pl.when(seg == segs - 1)
    def _():
        loaded(racts.at[pl.ds(0, width + qrows)], load_sem.at[1])
        l_top.wait()
        for n in range(HALVES):
            advance(n)

    pl.semaphore_wait(barrier, blks - 1 + segs - 1)

    @pl.when(seg == segs - 1)
    def _():
        for n in range(HALVES):
            e_copy(n).start()

    remote(acts_h.at[give, :], other_a, g1_send, sel_recv.at[0], seg, mate).start()
    remote(grads_h.at[give, :], other_g, g1_send, sel_recv.at[1], seg, mate).start()

    def send0(off, side):
        dest = chip_at(off) * 2 + side
        remote(
            grads_h.at[pl.ds(0, tb), cols(dest)],
            grads0.at[span(off * 2 + lane, tb)],
            g0_send,
            g0_recv.at[off],
            seg,
            dest,
        ).start()

    def send1(off, side):
        dest = chip_at(off) * 2 + side
        remote(
            own_g.at[:, cols(dest)],
            grads1.at[span(off * 2 + lane, half)],
            g1_send,
            g1_recv,
            seg,
            dest,
        ).start()

    near = list(low)
    far = [off for off in range(1, chips) if off not in near]
    for off in near:
        send0(off, lane)

    loaded(racts.at[pl.ds(0, width + rows)], load_sem.at[2])
    loaded(counts, load_sem.at[3])
    full = counts[blk] == SLOTS
    landed(other_a, sel_recv.at[0])
    acts[tb : tb + half] = jnp.where(
        full, acts[keep, :].astype(F32), other_a[...].astype(F32)
    ).astype(B16)
    mine = span(lane, block)
    racts[mine] = jnp.dot(acts[0:block], b_in[...], preferred_element_type=F32).astype(B16)

    def relay(code):
        slot = slot_of(code)
        src = racts_at(slot, lane)
        for j in range(code.bit_length(), steps):
            to = slot + bits[j]
            dest = partners[j] * 2 + lane
            remote(src, racts_at(to, lane), a_send, a_recv.at[to], seg, dest).start()
        remote(src, src, a_send, am_recv.at[slot], seg, mate).start()

    relay(0)
    for off in near:
        send0(off, mate_lane)
    for off in far:
        send0(off, lane)
        send0(off, mate_lane)
    send0(0, mate_lane)
    for off in range(1, segs):
        pl.semaphore_signal(
            ready, inc=1, device_id=(lax.rem(seg + off, segs), blk), device_id_type=MESH
        )

    loaded(own_g, load_sem.at[4])
    landed(other_g, sel_recv.at[1])
    own_g[...] = jnp.where(full, own_g[...].astype(F32), other_g[...].astype(F32)).astype(B16)

    @pl.when(seg < segs - 1)
    def _():
        loaded(racts.at[pl.ds(0, width + qrows)], load_sem.at[1])

    @pl.when(jnp.logical_and(seg > 0, seg < segs - 1))
    def _():
        for n in range(HALVES):
            landed(errs.at[pl.ds(n * piece, piece)], e_recv.at[n])
            advance(n)
            e_copy(n).start()

    for code in range(1, chips):
        if code.bit_length() == steps and code > 1 << steps - 1:
            continue
        landed(racts_at(slot_of(code), lane), a_recv.at[slot_of(code)])
        relay(code)
    for off in far + near:
        send1(off, lane)
        send1(off, mate_lane)
    send1(0, mate_lane)
    own1 = pltpu.make_async_copy(own_g.at[:, cols(blk)], grads1.at[span(lane, half)], g1_recv)
    own1.start()

    loaded(racts.at[pl.ds(0, width + qrows)], load_sem.at[5])
    rot_q[...] = jnp.dot(qacts[...], b_in[...], preferred_element_type=F32).astype(B16)
    loaded(eig, load_sem.at[6])
    inv = 1.0 / (eig[...].astype(F32) + damping)

    @pl.when(seg == 0)
    def _():
        for n in range(HALVES):
            landed(errs.at[pl.ds(n * piece, piece)], e_recv.at[n])

    rot_e = jnp.dot(errs[...], b_out[...], preferred_element_type=F32).astype(B16)
    for q in range(queries):
        r = slice(q * qt, (q + 1) * qt)
        raw = lax.dot_general(
            rot_e[r], rot_q[r], (((0,), (0,)), ((), ())), preferred_element_type=F32
        )
        core_all[:, q * width : (q + 1) * width] = (raw * inv).astype(B16)

    for code in range((1 << steps - 1) + 1, chips):
        landed(racts_at(slot_of(code), lane), a_recv.at[slot_of(code)])
        relay(code)

    def core_of(q):
        return core_all[:, q * width : (q + 1) * width]

    def folded(x):
        x = sum(x[:, n * 128 : (n + 1) * 128] for n in range(width // 128))
        return jnp.sum(x, axis=0, keepdims=True)

    def rows_of(i, side, start, size):
        return racts[pl.ds((i * 2 + side) * block + start, size), :].astype(F32)

    for pair in range(0, chips, 2):
        for i in (pair, pair + 1):
            landed(grads0.at[pl.ds(i * 2 * tb, 2 * tb)], g0_recv.at[i])
            landed(racts_at(i, mate_lane), am_recv.at[i])
        turned = jnp.dot(
            grads0[pl.ds(pair * 2 * tb, 4 * tb), :], b_out[...], preferred_element_type=F32
        ).astype(B16)
        for q in range(queries):
            h = jnp.dot(turned, core_of(q), preferred_element_type=F32)
            for n in range(4):
                i, side = pair + n // 2, n % 2
                prod = h[n * tb : (n + 1) * tb] * rows_of(i, side, 0, tb)
                part[i, side, q : q + 1, :] = folded(prod)

    landed(grads1, g1_recv)
    turned = jnp.dot(grads1[...], b_out[...], preferred_element_type=F32).astype(B16)
    for q in range(queries):
        h = jnp.dot(turned, core_of(q), preferred_element_type=F32)
        for i in range(chips):
            shared = sum(
                folded(
                    h[(i * 2 + side) * half : (i * 2 + side + 1) * half]
                    * rows_of(i, side, tb, half)
                )
                for side in range(2)
            )
            for side in range(2):
                part[i, side, queries + q : queries + q + 1, :] = shared

    values = SLOTS * queries
    tile = (chips, 2, values, 128)
    row = lax.broadcasted_iota(jnp.int32, tile, 2)
    col = lax.broadcasted_iota(jnp.int32, tile, 3)
    sums = jnp.sum(part[...], axis=3, keepdims=True)
    for s in range(SLOTS):
        placed = jnp.where(row == col + s * queries, sums, 0.0)
        placed = jnp.where(col < queries, placed, 0.0)
        packed[:, :, s : s + 1, :] = jnp.sum(placed, axis=2, keepdims=True)

    pl.semaphore_wait(ready, segs - 1)
    for seg_off in range(segs - 1, -1, -1):
        seg_to = lax.rem(seg + seg_off, segs)
        for off in range(chips - 1, -1, -1):
            chip_to = chip_at(off)
            for side in (lane, mate_lane):
                if seg_off == 0 and off == 0 and side is lane:
                    continue
                remote(
                    packed.at[off, side],
                    gathered.at[seg * blks + blk],
                    p_send,
                    p_recv,
                    seg_to,
                    chip_to * 2 + side,
                ).start()
    gathered[seg * blks + blk] = packed[0, lane]
    others = gathered.at[pl.ds(0, segs * blks - 1)]
    landed(others, p_recv)
    total = jnp.sum(gathered[...], axis=0)[:, 0:queries]
    slot = lax.broadcasted_iota(jnp.int32, total.shape, 0)
    out[...] = total * jnp.where(jnp.logical_or(slot == 0, full), 1.0, 0.0)

    remote(others, others, p_send, p_recv, seg, mate).wait_send()

    def sent(count, sem):
        ref = racts.at[pl.ds(0, count)]
        remote(ref, ref, sem, sel_recv.at[0], seg, mate).wait_send()

    sent((blks - 1) * tb, g0_send)
    sent((blks - 1) * half + half + half * blks, g1_send)
    sent((2 * chips - 1) * block, a_send)

    @pl.when(seg > 0)
    def _():
        sent(qrows, e_send)


def body(
    train_acts,
    train_grads,
    counts,
    basis_in,
    basis_out,
    eigenvalues,
    back_weight,
    derivative,
    query_acts,
    query_top,
):
    segs = lax.axis_size("seg")
    blks = lax.axis_size("blk")
    chips = blks // 2
    queries, qt, width = query_top.shape
    rows = train_acts.shape[1]
    tb = rows // SLOTS
    half = tb // 2
    wide = train_grads.shape[2]
    any_spec = pl.BlockSpec(memory_space=pltpu.HBM)
    vm = pltpu.VMEM
    dma = pltpu.SemaphoreType.DMA
    result = pl.pallas_call(
        functools.partial(kernel, segs, blks, queries),
        out_shape=pltpu.VMEM((SLOTS, queries), F32),
        in_specs=[any_spec] * 10,
        out_specs=pl.BlockSpec(memory_space=pltpu.VMEM),
        scratch_shapes=[
            pltpu.SMEM(counts.shape, counts.dtype),
            vm((rows, width), B16),
            vm((half, wide), B16),
            vm((half, wide), B16),
            vm((half, width), B16),
            vm((width, width), B16),
            vm((width, width), B16),
            vm((width, width), B16),
            vm((width, width), B16),
            vm((queries * qt, width), B16),
            vm((queries * qt, width), B16),
            vm((queries * qt, width), B16),
            vm((queries * qt, width), B16),
            vm((queries * qt, width), B16),
            vm((width, queries * width), B16),
            vm((blks * tb, width), B16),
            vm((blks * half, width), B16),
            vm((blks * (tb + half), width), B16),
            vm((chips, 2, SLOTS * queries, 128), F32),
            vm((chips, 2, SLOTS, 128), F32),
            vm((segs * blks, SLOTS, 128), F32),
            dma((7,)),
            dma((2,)),
            dma(()),
            dma((chips,)),
            dma(()),
            dma(()),
            dma(()),
            dma((chips,)),
            dma((chips,)),
            dma(()),
            dma((HALVES,)),
            dma(()),
            dma(()),
            pltpu.SemaphoreType.REGULAR,
        ],
        compiler_params=pltpu.CompilerParams(
            collective_id=0, has_side_effects=True, vmem_limit_bytes=67_043_328 - 32_768
        ),
    )(
        counts,
        train_acts[0],
        train_grads[0],
        basis_in[0, 0],
        basis_out[0, 0],
        eigenvalues[0, 0],
        back_weight[0, 0],
        derivative[0].reshape(queries * qt, width),
        query_acts[0].reshape(queries * qt, width),
        query_top.reshape(queries * qt, width),
    )
    return result.T


def solution(mesh):
    in_specs = (
        P("seg", "blk", None),
        P("seg", "blk", None),
        P(),
        P("seg", None, None, None),
        P("seg", "blk", None, None),
        P("seg", "blk", None, None),
        P("seg", "blk", None, None),
        P("seg", None, None, "blk"),
        P("seg", None, None, None),
        P(None, None, "blk"),
    )
    out_specs = P(None, "blk")
    return jax.shard_map(body, mesh=mesh, in_specs=in_specs, out_specs=out_specs, check_vma=False)
```

```python
import functools

import jax
import jax.numpy as jnp
from jax import lax
from jax.experimental import pallas as pl
from jax.experimental.pallas import tpu as pltpu
from jax.sharding import PartitionSpec as P

SLOTS = 2
damping = 0.05
F32 = jnp.float32
B16 = jnp.bfloat16
MESH = pl.DeviceIdType.MESH


def kernel(
    segs,
    blks,
    queries,
    counts_h,
    acts_h,
    grads_h,
    bin_h,
    bout_h,
    eig_h,
    back_h,
    deriv_h,
    qacts_h,
    qtop_h,
    out,
    counts,
    acts,
    own_g,
    other_g,
    other_a,
    b_in,
    b_out,
    eig,
    back,
    deriv,
    qacts,
    errs,
    moved,
    rot_q,
    core_all,
    grads0,
    grads1,
    racts0,
    racts1,
    part,
    packed,
    gathered,
    load_sem,
    sel_recv,
    g0_send,
    g1_send,
    a_send,
    early_recv,
    late_recv,
    a0_recv,
    a1_recv,
    e_send,
    e_recv,
    p_send,
    p_recv,
    ready,
):
    seg = lax.axis_index("seg")
    blk = lax.axis_index("blk")
    chips = blks // 2
    steps = chips.bit_length() - 1
    chip = blk // 2
    lane = blk % 2
    mate_lane = 1 - lane
    mate = chip * 2 + mate_lane
    rows = acts_h.shape[0]
    tb = rows // SLOTS
    half = tb // 2
    width = bin_h.shape[0]
    qrows = qtop_h.shape[0]
    qt = qrows // queries

    barrier = pltpu.get_barrier_semaphore()
    for off in range(1, blks):
        pl.semaphore_signal(
            barrier, inc=1, device_id=(seg, lax.rem(blk + off, blks)), device_id_type=MESH
        )
    above, below = lax.rem(seg + 1, segs), lax.rem(seg + segs - 1, segs)

    @pl.when(seg < segs - 1)
    def _():
        pl.semaphore_signal(barrier, inc=1, device_id=(above, blk), device_id_type=MESH)

    @pl.when(seg > 0)
    def _():
        pl.semaphore_signal(barrier, inc=1, device_id=(below, blk), device_id_type=MESH)

    def flip(c, bit):
        return c + bit * (1 - 2 * lax.rem(c // bit, 2))

    def chip_at(off):
        c = chip
        for j in range(steps):
            if off >> j & 1:
                c = flip(c, 1 << j)
        return c

    low = [1 << j for j in range(steps)]
    high = low[::-1]
    bits = [a + lane * (b - a) for a, b in zip(low, high)]
    partners = [flip(chip, a) + lane * (flip(chip, b) - flip(chip, a)) for a, b in zip(low, high)]

    def slot_of(code):
        return sum((bits[j] for j in range(steps) if code >> j & 1), 0)

    def remote(src, dst, ssem, rsem, seg_to, blk_to):
        return pltpu.make_async_remote_copy(
            src_ref=src,
            dst_ref=dst,
            send_sem=ssem,
            recv_sem=rsem,
            device_id=(seg_to, blk_to),
            device_id_type=MESH,
        )

    def cols(index):
        return pl.ds(pl.multiple_of(index * width, width), width)

    def span(index, size):
        return pl.ds(pl.multiple_of(index * size, size), size)

    def landed(ref, sem):
        remote(ref, ref, g0_send, sem, seg, mate).wait_recv()

    def loaded(ref, sem):
        pltpu.make_async_copy(ref, ref, sem).wait()

    racts = (racts0, racts1)
    a_recv = (a0_recv, a1_recv)

    def racts_at(slot, side, part_of):
        return racts[part_of].at[span(slot * 2 + side, tb if part_of == 0 else half)]

    def bulk(count):
        return core_all.at[pl.ds(0, count // 2), 0 : 2 * width]

    keep = pl.ds(pl.multiple_of(tb + lane * half, half), half)
    give = pl.ds(pl.multiple_of(tb + mate_lane * half, half), half)

    l_top = pltpu.make_async_copy(qtop_h, errs, load_sem.at[0])

    @pl.when(seg == segs - 1)
    def _():
        l_top.start()

    for src, dst, n in (
        (acts_h, acts, 2),
        (bin_h, b_in, 2),
        (back_h, back, 1),
        (deriv_h, deriv, 1),
        (counts_h, counts, 3),
        (grads_h.at[keep, :], own_g, 4),
        (bout_h, b_out, 5),
        (qacts_h, qacts, 5),
        (eig_h, eig, 6),
        (grads_h.at[pl.ds(0, tb), cols(blk)], grads0.at[span(lane, tb)], None),
    ):
        sem = early_recv.at[0] if n is None else load_sem.at[n]
        pltpu.make_async_copy(src, dst, sem).start()

    def e_copy(n):
        r = pl.ds(n * qt, qt)
        return remote(moved.at[r], errs.at[r], e_send, e_recv.at[n], below, blk)

    def advance(n):
        r = pl.ds(n * qt, qt)
        e = errs[r]
        mixed = jnp.dot(e, back[...], preferred_element_type=F32)
        moved[r] = (e.astype(F32) + mixed * deriv[r].astype(F32)).astype(B16)

    def relay(code, part_of):
        slot = slot_of(code)
        src = racts_at(slot, lane, part_of)
        for j in range(code.bit_length(), steps):
            to = slot + bits[j]
            dst, dest = racts_at(to, lane, part_of), partners[j] * 2 + lane
            remote(src, dst, a_send.at[part_of], a_recv[part_of].at[to], seg, dest).start()
        sem = late_recv if part_of else early_recv.at[slot]
        remote(src, src, a_send.at[part_of], sem, seg, mate).start()

    def handed_on(code, part_of):
        slot = slot_of(code)
        landed(racts_at(slot, lane, part_of), a_recv[part_of].at[slot])
        relay(code, part_of)

    def send0(off, chip_to, side):
        dest = chip_to * 2 + side
        remote(
            grads_h.at[pl.ds(0, tb), cols(dest)],
            grads0.at[span(off * 2 + lane, tb)],
            g0_send,
            early_recv.at[off],
            seg,
            dest,
        ).start()

    def send1(off, side):
        dest = chip_at(off) * 2 + side
        remote(
            own_g.at[:, cols(dest)],
            grads1.at[span(off * 2 + lane, half)],
            g1_send,
            late_recv,
            seg,
            dest,
        ).start()

    near = list(low)
    far = [off for off in range(1, chips) if off not in near]
    last_codes = list(range((1 << steps - 1) + 1, chips))
    first_codes = [code for code in range(1, chips) if code not in last_codes]

    loaded(bulk(width + rows), load_sem.at[2])
    racts0[span(lane, tb)] = jnp.dot(
        acts[0:tb], b_in[...], preferred_element_type=F32
    ).astype(B16)

    @pl.when(seg == segs - 1)
    def _():
        loaded(bulk(width + qrows), load_sem.at[1])
        l_top.wait()
        for n in range(queries // 2):
            advance(n)

    sides = (seg + segs - 1) // segs + (2 * segs - 2 - seg) // segs
    pl.semaphore_wait(barrier, blks - 1 + sides)

    remote(acts_h.at[give, :], other_a, g1_send, sel_recv.at[0], seg, mate).start()
    relay(0, 0)
    remote(grads_h.at[give, :], other_g, g1_send, sel_recv.at[1], seg, mate).start()

    @pl.when(seg == segs - 1)
    def _():
        for n in range(queries // 2):
            e_copy(n).start()
        for n in range(queries // 2, queries):
            advance(n)
            e_copy(n).start()

    loaded(counts, load_sem.at[3])
    full = counts[blk] == SLOTS
    landed(other_a, sel_recv.at[0])
    picked = jnp.where(full, acts[keep, :].astype(F32), other_a[...].astype(F32)).astype(B16)
    racts1[span(lane, half)] = jnp.dot(picked, b_in[...], preferred_element_type=F32).astype(B16)

    relay(0, 1)
    for j in range(steps - 1):
        send0(bits[j], partners[j], lane)
        send0(bits[j], partners[j], mate_lane)

    def tell_above():
        pl.semaphore_signal(ready, inc=1, device_id=(above, blk), device_id_type=MESH)

    pl.when(seg == 0)(tell_above)

    loaded(own_g, load_sem.at[4])
    landed(other_g, sel_recv.at[1])
    own_g[...] = jnp.where(full, own_g[...].astype(F32), other_g[...].astype(F32)).astype(B16)

    for code in first_codes:
        handed_on(code, 0)
    for code in first_codes:
        handed_on(code, 1)
    send0(bits[steps - 1], partners[steps - 1], lane)
    send0(bits[steps - 1], partners[steps - 1], mate_lane)
    for off in far:
        send0(off, chip_at(off), lane)
        send0(off, chip_at(off), mate_lane)
    send0(0, chip, mate_lane)
    for off in far + near:
        send1(off, lane)
        send1(off, mate_lane)
    send1(0, mate_lane)
    own1 = pltpu.make_async_copy(own_g.at[:, cols(blk)], grads1.at[span(lane, half)], late_recv)
    own1.start()

    @pl.when(jnp.logical_and(seg > 0, seg < segs - 1))
    def _():
        pl.semaphore_wait(ready, 1)
        tell_above()

    @pl.when(seg < segs - 1)
    def _():
        loaded(bulk(width + qrows), load_sem.at[1])

    @pl.when(jnp.logical_and(seg > 0, seg < segs - 1))
    def _():
        for n in range(queries):
            landed(errs.at[pl.ds(n * qt, qt)], e_recv.at[n])
            advance(n)
            e_copy(n).start()

    loaded(bulk(width + qrows), load_sem.at[5])
    rot_q[...] = jnp.dot(qacts[...], b_in[...], preferred_element_type=F32).astype(B16)
    loaded(eig, load_sem.at[6])
    inv = 1.0 / (eig[...].astype(F32) + damping)

    def relay_last():
        for code in last_codes:
            handed_on(code, 0)
            handed_on(code, 1)

    pl.when(seg == 0)(relay_last)

    for q in range(queries):

        @pl.when(seg == 0)
        def _():
            landed(errs.at[pl.ds(q * qt, qt)], e_recv.at[q])

        r = pl.ds(q * qt, qt)
        rot_e = jnp.dot(errs[r], b_out[...], preferred_element_type=F32).astype(B16)
        raw = lax.dot_general(
            rot_e, rot_q[r], (((0,), (0,)), ((), ())), preferred_element_type=F32
        )
        core_all[:, q * width : (q + 1) * width] = (raw * inv).astype(B16)

    pl.when(seg > 0)(relay_last)

    def core_of(q):
        return core_all[:, q * width : (q + 1) * width]

    def folded(x):
        x = sum(x[:, n * 128 : (n + 1) * 128] for n in range(width // 128))
        return jnp.sum(x, axis=0, keepdims=True)

    for pair in range(0, chips, 2):
        for i in (pair, pair + 1):
            landed(grads0.at[pl.ds(0, 3 * tb)], early_recv.at[i])
        here = pl.ds(pair * 2 * tb, 4 * tb)
        turned = jnp.dot(grads0[here, :], b_out[...], preferred_element_type=F32).astype(B16)
        for q in range(queries):
            h = jnp.dot(turned, core_of(q), preferred_element_type=F32)
            prod = h * racts0[here, :].astype(F32)
            for n in range(4):
                i, side = pair + n // 2, n % 2
                part[i, side, q : q + 1, :] = folded(prod[n * tb : (n + 1) * tb])

    landed(racts0.at[pl.ds(0, (blks + chips) * half)], late_recv)
    turned = jnp.dot(grads1[...], b_out[...], preferred_element_type=F32).astype(B16)
    for q in range(queries):
        h = jnp.dot(turned, core_of(q), preferred_element_type=F32)
        prod = h * racts1[...].astype(F32)
        for i in range(chips):
            shared = folded(prod[i * tb : (i + 1) * tb])
            for side in range(2):
                part[i, side, queries + q : queries + q + 1, :] = shared

    values = SLOTS * queries
    tile = (chips, 2, values, 128)
    diag = lax.broadcasted_iota(jnp.int32, tile, 2) == lax.broadcasted_iota(jnp.int32, tile, 3)
    sums = jnp.sum(part[...], axis=3, keepdims=True)
    packed[...] = jnp.sum(jnp.where(diag, sums, 0.0), axis=2, keepdims=True)

    @pl.when(seg == segs - 1)
    def _():
        pl.semaphore_wait(ready, 1)

    for seg_off in range(segs - 1, -1, -1):
        seg_to = lax.rem(seg + seg_off, segs)
        for off in range(chips - 1, -1, -1):
            chip_to = chip_at(off)
            for side in (lane, mate_lane):
                if seg_off == 0 and off == 0 and side is lane:
                    continue
                remote(
                    packed.at[off, side],
                    gathered.at[seg * blks + blk],
                    p_send,
                    p_recv,
                    seg_to,
                    chip_to * 2 + side,
                ).start()
    gathered[seg * blks + blk] = packed[0, lane]
    others = gathered.at[pl.ds(0, segs * blks - 1)]
    landed(others, p_recv)
    total = jnp.sum(gathered[...].reshape(segs * blks, 128), axis=0, keepdims=True)
    tile = (values, 128)
    row = lax.broadcasted_iota(jnp.int32, tile, 0)
    col = lax.broadcasted_iota(jnp.int32, tile, 1)
    spread = jnp.where(row == col, jnp.broadcast_to(total, tile), 0.0)
    spread = jnp.sum(spread, axis=1, keepdims=True)
    spread = jnp.where(lax.rem(row, queries) == col, jnp.broadcast_to(spread, tile), 0.0)
    for n in range(SLOTS):
        scores = jnp.sum(
            jnp.where(row // queries == n, spread, 0.0), axis=0, keepdims=True
        )[:, 0:queries]
        out[n : n + 1, :] = scores * jnp.where(full, 1.0, 0.0) if n else scores

    remote(others, others, p_send, p_recv, seg, mate).wait_send()

    def sent(count, sem):
        ref = racts0.at[pl.ds(0, count)]
        remote(ref, ref, sem, sel_recv.at[0], seg, mate).wait_send()

    sent((blks - 1) * tb, g0_send)
    sent((blks - 1) * half + half + half * blks, g1_send)
    sent((2 * chips - 1) * tb, a_send.at[0])
    sent((2 * chips - 1) * half, a_send.at[1])

    @pl.when(seg > 0)
    def _():
        sent(qrows, e_send)


def body(
    train_acts,
    train_grads,
    counts,
    basis_in,
    basis_out,
    eigenvalues,
    back_weight,
    derivative,
    query_acts,
    query_top,
):
    segs = lax.axis_size("seg")
    blks = lax.axis_size("blk")
    chips = blks // 2
    queries, qt, width = query_top.shape
    rows = train_acts.shape[1]
    tb = rows // SLOTS
    half = tb // 2
    wide = train_grads.shape[2]
    any_spec = pl.BlockSpec(memory_space=pltpu.HBM)
    vm = pltpu.VMEM
    dma = pltpu.SemaphoreType.DMA
    result = pl.pallas_call(
        functools.partial(kernel, segs, blks, queries),
        out_shape=pltpu.VMEM((SLOTS, queries), F32),
        in_specs=[any_spec] * 10,
        out_specs=pl.BlockSpec(memory_space=pltpu.VMEM),
        scratch_shapes=[
            pltpu.SMEM(counts.shape, counts.dtype),
            vm((rows, width), B16),
            vm((half, wide), B16),
            vm((half, wide), B16),
            vm((half, width), B16),
            vm((width, width), B16),
            vm((width, width), B16),
            vm((width, width), B16),
            vm((width, width), B16),
            vm((queries * qt, width), B16),
            vm((queries * qt, width), B16),
            vm((queries * qt, width), B16),
            vm((queries * qt, width), B16),
            vm((queries * qt, width), B16),
            vm((width, queries * width), B16),
            vm((blks * tb, width), B16),
            vm((blks * half, width), B16),
            vm((blks * tb, width), B16),
            vm((blks * half, width), B16),
            vm((chips, 2, SLOTS * queries, 128), F32),
            vm((chips, 2, 1, 128), F32),
            vm((segs * blks, 1, 128), F32),
            dma((7,)),
            dma((2,)),
            dma(()),
            dma(()),
            dma((2,)),
            dma((chips,)),
            dma(()),
            dma((chips,)),
            dma((chips,)),
            dma(()),
            dma((queries,)),
            dma(()),
            dma(()),
            pltpu.SemaphoreType.REGULAR,
        ],
        compiler_params=pltpu.CompilerParams(
            collective_id=0, has_side_effects=True, vmem_limit_bytes=67_043_328 - 32_768
        ),
    )(
        counts,
        train_acts[0],
        train_grads[0],
        basis_in[0, 0],
        basis_out[0, 0],
        eigenvalues[0, 0],
        back_weight[0, 0],
        derivative[0].reshape(queries * qt, width),
        query_acts[0].reshape(queries * qt, width),
        query_top.reshape(queries * qt, width),
    )
    return result.T


def solution(mesh):
    in_specs = (
        P("seg", "blk", None),
        P("seg", "blk", None),
        P(),
        P("seg", None, None, None),
        P("seg", "blk", None, None),
        P("seg", "blk", None, None),
        P("seg", "blk", None, None),
        P("seg", None, None, "blk"),
        P("seg", None, None, None),
        P(None, None, "blk"),
    )
    out_specs = P(None, "blk")
    return jax.shard_map(body, mesh=mesh, in_specs=in_specs, out_specs=out_specs, check_vma=False)
```

```python
import functools

import jax
import jax.numpy as jnp
from jax import lax
from jax.experimental import pallas as pl
from jax.experimental.pallas import tpu as pltpu
from jax.sharding import PartitionSpec as P

SLOTS = 2
damping = 0.05
F32 = jnp.float32
B16 = jnp.bfloat16
MESH = pl.DeviceIdType.MESH


def kernel(
    segs,
    blks,
    queries,
    counts_h,
    acts_h,
    grads_h,
    bin_h,
    bout_h,
    eig_h,
    back_h,
    deriv_h,
    qacts_h,
    qtop_h,
    out,
    counts,
    acts,
    own_g,
    other_g,
    other_a,
    b_in,
    b_out,
    eig,
    back,
    deriv,
    qacts,
    errs,
    moved,
    rot_q,
    core_all,
    grads0,
    grads1,
    racts0,
    racts1,
    part,
    packed,
    gathered,
    load_sem,
    sel_recv,
    g0_send,
    g1_send,
    a_send,
    early_recv,
    late_recv,
    a0_recv,
    a1_recv,
    e_send,
    e_recv,
    p_send,
    p_recv,
    ready,
):
    seg = lax.axis_index("seg")
    blk = lax.axis_index("blk")
    chips = blks // 2
    steps = chips.bit_length() - 1
    chip = blk // 2
    lane = blk % 2
    mate_lane = 1 - lane
    mate = chip * 2 + mate_lane
    rows = acts_h.shape[0]
    tb = rows // SLOTS
    half = tb // 2
    width = bin_h.shape[0]
    qrows = qtop_h.shape[0]
    qt = qrows // queries

    barrier = pltpu.get_barrier_semaphore()
    for off in range(1, blks):
        pl.semaphore_signal(
            barrier, inc=1, device_id=(seg, lax.rem(blk + off, blks)), device_id_type=MESH
        )
    above, below = lax.rem(seg + 1, segs), lax.rem(seg + segs - 1, segs)

    @pl.when(seg < segs - 1)
    def _():
        pl.semaphore_signal(barrier, inc=1, device_id=(above, blk), device_id_type=MESH)

    @pl.when(seg > 0)
    def _():
        pl.semaphore_signal(barrier, inc=1, device_id=(below, blk), device_id_type=MESH)

    def flip(c, bit):
        return c + bit * (1 - 2 * lax.rem(c // bit, 2))

    def chip_at(off):
        c = chip
        for j in range(steps):
            if off >> j & 1:
                c = flip(c, 1 << j)
        return c

    low = [1 << j for j in range(steps)]
    high = low[::-1]
    bits = [a + lane * (b - a) for a, b in zip(low, high)]
    partners = [flip(chip, a) + lane * (flip(chip, b) - flip(chip, a)) for a, b in zip(low, high)]

    def slot_of(code):
        return sum((bits[j] for j in range(steps) if code >> j & 1), 0)

    def remote(src, dst, ssem, rsem, seg_to, blk_to):
        return pltpu.make_async_remote_copy(
            src_ref=src,
            dst_ref=dst,
            send_sem=ssem,
            recv_sem=rsem,
            device_id=(seg_to, blk_to),
            device_id_type=MESH,
        )

    def cols(index):
        return pl.ds(pl.multiple_of(index * width, width), width)

    def span(index, size):
        return pl.ds(pl.multiple_of(index * size, size), size)

    def landed(ref, sem):
        remote(ref, ref, g0_send, sem, seg, mate).wait_recv()

    def loaded(ref, sem):
        pltpu.make_async_copy(ref, ref, sem).wait()

    racts = (racts0, racts1)
    a_recv = (a0_recv, a1_recv)

    def racts_at(slot, side, part_of):
        return racts[part_of].at[span(slot * 2 + side, tb if part_of == 0 else half)]

    def bulk(count):
        return core_all.at[pl.ds(0, count // 2), 0 : 2 * width]

    keep = pl.ds(pl.multiple_of(tb + lane * half, half), half)
    give = pl.ds(pl.multiple_of(tb + mate_lane * half, half), half)

    def load(src, dst, sem):
        pltpu.make_async_copy(src, dst, sem).start()

    load(acts_h, acts, load_sem.at[2])
    load(bin_h, b_in, load_sem.at[2])
    load(counts_h, counts, load_sem.at[3])
    load(grads_h.at[keep, :], own_g, load_sem.at[4])

    @pl.when(seg == segs - 1)
    def _():
        load(back_h, back, load_sem.at[1])
        load(deriv_h, deriv, load_sem.at[1])
        load(qtop_h, errs, load_sem.at[0])

    def e_copy(n):
        r = pl.ds(n * qt, qt)
        return remote(moved.at[r], errs.at[r], e_send, e_recv.at[n], below, blk)

    def advance(n):
        r = pl.ds(n * qt, qt)
        e = errs[r]
        mixed = jnp.dot(e, back[...], preferred_element_type=F32)
        moved[r] = (e.astype(F32) + mixed * deriv[r].astype(F32)).astype(B16)

    def relay(code, part_of):
        slot = slot_of(code)
        src = racts_at(slot, lane, part_of)
        for j in range(code.bit_length(), steps):
            to = slot + bits[j]
            dst, dest = racts_at(to, lane, part_of), partners[j] * 2 + lane
            remote(src, dst, a_send.at[part_of], a_recv[part_of].at[to], seg, dest).start()
        sem = late_recv if part_of else early_recv.at[slot]
        remote(src, src, a_send.at[part_of], sem, seg, mate).start()

    def handed_on(code, part_of):
        slot = slot_of(code)
        landed(racts_at(slot, lane, part_of), a_recv[part_of].at[slot])
        relay(code, part_of)

    def send0(off, chip_to, side):
        dest = chip_to * 2 + side
        remote(
            grads_h.at[pl.ds(0, tb), cols(dest)],
            grads0.at[span(off * 2 + lane, tb)],
            g0_send,
            early_recv.at[off],
            seg,
            dest,
        ).start()

    def send1(off, side):
        dest = chip_at(off) * 2 + side
        remote(
            own_g.at[:, cols(dest)],
            grads1.at[span(off * 2 + lane, half)],
            g1_send,
            late_recv,
            seg,
            dest,
        ).start()

    near = list(low)
    far = [off for off in range(1, chips) if off not in near]
    last_codes = list(range((1 << steps - 1) + 1, chips))
    first_codes = [code for code in range(1, chips) if code not in last_codes]

    loaded(bulk(width + rows), load_sem.at[2])
    racts0[span(lane, tb)] = jnp.dot(
        acts[0:tb], b_in[...], preferred_element_type=F32
    ).astype(B16)

    sides = (seg + segs - 1) // segs + (2 * segs - 2 - seg) // segs
    pl.semaphore_wait(barrier, blks - 1 + sides)

    remote(acts_h.at[give, :], other_a, g1_send, sel_recv.at[0], seg, mate).start()
    relay(0, 0)
    remote(grads_h.at[give, :], other_g, g1_send, sel_recv.at[1], seg, mate).start()

    @pl.when(seg == segs - 1)
    def _():
        loaded(bulk(width + qrows), load_sem.at[1])
        loaded(errs, load_sem.at[0])
        for n in range(queries):
            advance(n)
            e_copy(n).start()

    @pl.when(seg < segs - 1)
    def _():
        load(back_h, back, load_sem.at[1])
        load(deriv_h, deriv, load_sem.at[1])

    load(bout_h, b_out, load_sem.at[5])
    load(qacts_h, qacts, load_sem.at[5])
    load(eig_h, eig, load_sem.at[6])
    load(grads_h.at[pl.ds(0, tb), cols(blk)], grads0.at[span(lane, tb)], early_recv.at[0])

    loaded(counts, load_sem.at[3])
    full = counts[blk] == SLOTS
    landed(other_a, sel_recv.at[0])
    picked = jnp.where(full, acts[keep, :].astype(F32), other_a[...].astype(F32)).astype(B16)
    racts1[span(lane, half)] = jnp.dot(picked, b_in[...], preferred_element_type=F32).astype(B16)

    relay(0, 1)
    for j in range(steps - 1):
        send0(bits[j], partners[j], lane)
        send0(bits[j], partners[j], mate_lane)

    def tell_above():
        pl.semaphore_signal(ready, inc=1, device_id=(above, blk), device_id_type=MESH)

    pl.when(seg == 0)(tell_above)

    loaded(own_g, load_sem.at[4])
    landed(other_g, sel_recv.at[1])
    own_g[...] = jnp.where(full, own_g[...].astype(F32), other_g[...].astype(F32)).astype(B16)

    def chain():
        loaded(bulk(width + qrows), load_sem.at[1])
        for n in range(queries):
            landed(errs.at[pl.ds(n * qt, qt)], e_recv.at[n])
            advance(n)
            e_copy(n).start()

    for code in first_codes:
        handed_on(code, 0)
    for code in first_codes:
        handed_on(code, 1)
    for side in (lane, mate_lane):
        for off in far:
            send0(off, chip_at(off), side)
        send0(bits[steps - 1], partners[steps - 1], side)
    send0(0, chip, mate_lane)
    for off in far + near:
        send1(off, lane)
        send1(off, mate_lane)
    send1(0, mate_lane)
    own1 = pltpu.make_async_copy(own_g.at[:, cols(blk)], grads1.at[span(lane, half)], late_recv)
    own1.start()

    @pl.when(jnp.logical_and(seg > 0, seg < segs - 1))
    def _():
        pl.semaphore_wait(ready, 1)
        tell_above()

    pl.when(jnp.logical_and(seg > 0, seg < segs - 1))(chain)

    @pl.when(seg == 0)
    def _():
        loaded(bulk(width + qrows), load_sem.at[1])

    loaded(bulk(width + qrows), load_sem.at[5])
    rot_q[...] = jnp.dot(qacts[...], b_in[...], preferred_element_type=F32).astype(B16)
    loaded(eig, load_sem.at[6])
    inv = 1.0 / (eig[...].astype(F32) + damping)

    def relay_last():
        for code in last_codes:
            handed_on(code, 0)
            handed_on(code, 1)

    pl.when(seg == 0)(relay_last)

    for q in range(queries):

        @pl.when(seg == 0)
        def _():
            landed(errs.at[pl.ds(q * qt, qt)], e_recv.at[q])

        r = pl.ds(q * qt, qt)
        rot_e = jnp.dot(errs[r], b_out[...], preferred_element_type=F32).astype(B16)
        raw = lax.dot_general(
            rot_e, rot_q[r], (((0,), (0,)), ((), ())), preferred_element_type=F32
        )
        core_all[:, q * width : (q + 1) * width] = (raw * inv).astype(B16)

    pl.when(seg > 0)(relay_last)

    def core_of(q):
        return core_all[:, q * width : (q + 1) * width]

    def folded(x):
        x = sum(x[:, n * 128 : (n + 1) * 128] for n in range(width // 128))
        return jnp.sum(x, axis=0, keepdims=True)

    for pair in range(0, chips, 2):
        for i in (pair, pair + 1):
            landed(grads0.at[pl.ds(0, 3 * tb)], early_recv.at[i])
        here = pl.ds(pair * 2 * tb, 4 * tb)
        turned = jnp.dot(grads0[here, :], b_out[...], preferred_element_type=F32).astype(B16)
        for q in range(queries):
            h = jnp.dot(turned, core_of(q), preferred_element_type=F32)
            prod = h * racts0[here, :].astype(F32)
            for n in range(4):
                i, side = pair + n // 2, n % 2
                part[i, side, q : q + 1, :] = folded(prod[n * tb : (n + 1) * tb])

    landed(racts0.at[pl.ds(0, (blks + chips) * half)], late_recv)
    turned = jnp.dot(grads1[...], b_out[...], preferred_element_type=F32).astype(B16)
    for q in range(queries):
        h = jnp.dot(turned, core_of(q), preferred_element_type=F32)
        prod = h * racts1[...].astype(F32)
        for i in range(chips):
            shared = folded(prod[i * tb : (i + 1) * tb])
            for side in range(2):
                part[i, side, queries + q : queries + q + 1, :] = shared

    values = SLOTS * queries
    tile = (chips, 2, values, 128)
    diag = lax.broadcasted_iota(jnp.int32, tile, 2) == lax.broadcasted_iota(jnp.int32, tile, 3)
    sums = jnp.sum(part[...], axis=3, keepdims=True)
    packed[...] = jnp.sum(jnp.where(diag, sums, 0.0), axis=2, keepdims=True)

    @pl.when(seg == segs - 1)
    def _():
        pl.semaphore_wait(ready, 1)

    for seg_off in range(segs - 1, -1, -1):
        seg_to = lax.rem(seg + seg_off, segs)
        for off in range(chips - 1, -1, -1):
            chip_to = chip_at(off)
            for side in (lane, mate_lane):
                if seg_off == 0 and off == 0 and side is lane:
                    continue
                remote(
                    packed.at[off, side],
                    gathered.at[seg * blks + blk],
                    p_send,
                    p_recv,
                    seg_to,
                    chip_to * 2 + side,
                ).start()
    gathered[seg * blks + blk] = packed[0, lane]
    others = gathered.at[pl.ds(0, segs * blks - 1)]
    landed(others, p_recv)
    total = jnp.sum(gathered[...].reshape(segs * blks, 128), axis=0, keepdims=True)
    tile = (values, 128)
    row = lax.broadcasted_iota(jnp.int32, tile, 0)
    col = lax.broadcasted_iota(jnp.int32, tile, 1)
    spread = jnp.where(row == col, jnp.broadcast_to(total, tile), 0.0)
    spread = jnp.sum(spread, axis=1, keepdims=True)
    spread = jnp.where(lax.rem(row, queries) == col, jnp.broadcast_to(spread, tile), 0.0)
    for n in range(SLOTS):
        scores = jnp.sum(
            jnp.where(row // queries == n, spread, 0.0), axis=0, keepdims=True
        )[:, 0:queries]
        out[n : n + 1, :] = scores * jnp.where(full, 1.0, 0.0) if n else scores

    remote(others, others, p_send, p_recv, seg, mate).wait_send()

    def sent(count, sem):
        ref = racts0.at[pl.ds(0, count)]
        remote(ref, ref, sem, sel_recv.at[0], seg, mate).wait_send()

    sent((blks - 1) * tb, g0_send)
    sent((blks - 1) * half + half + half * blks, g1_send)
    sent((2 * chips - 1) * tb, a_send.at[0])
    sent((2 * chips - 1) * half, a_send.at[1])

    @pl.when(seg > 0)
    def _():
        sent(qrows, e_send)


def body(
    train_acts,
    train_grads,
    counts,
    basis_in,
    basis_out,
    eigenvalues,
    back_weight,
    derivative,
    query_acts,
    query_top,
):
    segs = lax.axis_size("seg")
    blks = lax.axis_size("blk")
    chips = blks // 2
    queries, qt, width = query_top.shape
    rows = train_acts.shape[1]
    tb = rows // SLOTS
    half = tb // 2
    wide = train_grads.shape[2]
    any_spec = pl.BlockSpec(memory_space=pltpu.HBM)
    vm = pltpu.VMEM
    dma = pltpu.SemaphoreType.DMA
    result = pl.pallas_call(
        functools.partial(kernel, segs, blks, queries),
        out_shape=pltpu.VMEM((SLOTS, queries), F32),
        in_specs=[any_spec] * 10,
        out_specs=pl.BlockSpec(memory_space=pltpu.VMEM),
        scratch_shapes=[
            pltpu.SMEM(counts.shape, counts.dtype),
            vm((rows, width), B16),
            vm((half, wide), B16),
            vm((half, wide), B16),
            vm((half, width), B16),
            vm((width, width), B16),
            vm((width, width), B16),
            vm((width, width), B16),
            vm((width, width), B16),
            vm((queries * qt, width), B16),
            vm((queries * qt, width), B16),
            vm((queries * qt, width), B16),
            vm((queries * qt, width), B16),
            vm((queries * qt, width), B16),
            vm((width, queries * width), B16),
            vm((blks * tb, width), B16),
            vm((blks * half, width), B16),
            vm((blks * tb, width), B16),
            vm((blks * half, width), B16),
            vm((chips, 2, SLOTS * queries, 128), F32),
            vm((chips, 2, 1, 128), F32),
            vm((segs * blks, 1, 128), F32),
            dma((7,)),
            dma((2,)),
            dma(()),
            dma(()),
            dma((2,)),
            dma((chips,)),
            dma(()),
            dma((chips,)),
            dma((chips,)),
            dma(()),
            dma((queries,)),
            dma(()),
            dma(()),
            pltpu.SemaphoreType.REGULAR,
        ],
        compiler_params=pltpu.CompilerParams(
            collective_id=0, has_side_effects=True, vmem_limit_bytes=67_043_328 - 32_768
        ),
    )(
        counts,
        train_acts[0],
        train_grads[0],
        basis_in[0, 0],
        basis_out[0, 0],
        eigenvalues[0, 0],
        back_weight[0, 0],
        derivative[0].reshape(queries * qt, width),
        query_acts[0].reshape(queries * qt, width),
        query_top.reshape(queries * qt, width),
    )
    return result.T


def solution(mesh):
    in_specs = (
        P("seg", "blk", None),
        P("seg", "blk", None),
        P(),
        P("seg", None, None, None),
        P("seg", "blk", None, None),
        P("seg", "blk", None, None),
        P("seg", "blk", None, None),
        P("seg", None, None, "blk"),
        P("seg", None, None, None),
        P(None, None, "blk"),
    )
    out_specs = P(None, "blk")
    return jax.shard_map(body, mesh=mesh, in_specs=in_specs, out_specs=out_specs, check_vma=False)
```
